256 devices in a mesh: section: 4 (over y), ctx: 16 (over z, x_hi), tp: 4 (over x_lo, core).
Axes of the slice: x: 4 (x_hi: 2, x_lo: 2; x = x_hi * 2 + x_lo), y: 4, z: 8, core: 2. Of those that a mesh axis runs over, the one named last changes fastest.
Arguments:
- hidden_in: bfloat16 [4, 2048, 4096], P('section', 'ctx', 'tp'), may hold values from -16 to 16
- fresh_in: bfloat16 [3, 2048, 4096], P(None, 'ctx', 'tp'), may hold values from -16 to 16
- block_table: int32 [32], replicated, may hold values from 0 to 31, as said below
- norm_gain: float32 [4, 4096], P('section'), may hold values from 0.1 to 1.9
- w_query: bfloat16 [4, 4096, 4096], P('section', 'ctx', 'tp'), may hold values from -3.125 to 3.125
- w_key: bfloat16 [4, 4096, 512], P('section', 'ctx', 'tp'), may hold values from -0.09375 to 0.09375
- w_value: bfloat16 [4, 4096, 512], P('section', 'ctx', 'tp'), may hold values from -0.09375 to 0.09375
- w_out: bfloat16 [4, 4096, 4096], P('section', 'ctx', 'tp'), may hold values from -0.09375 to 0.09375
Outputs:
- layer_outputs: bfloat16 [4, 4, 2048, 4096], P(None, 'section', 'ctx', 'tp')
The draws below stay inside these ranges and needn't reach their ends.
Inputs may be any that keep to these rules, and one draw needn't show every extreme that they name: `block_table`: slots 2i and 2i + 1 hold blocks p and 31 - p for some p, in either order; every block appears once.
All inputs are finite; a program needn't handle non-finite values.
Results may differ from the reference program's by a relative error of at most 0.03.
Values may be sent and summed in bfloat16 or wider, within the bound.
No kernel may reach another device: no remote copies, remote signals or barrier semaphores. Data moves between devices by JAX's collectives and lax.ppermute only.
A program may use at most 128 MiB of HBM per device.

```python
import jax
import jax.numpy as jnp
from jax import lax

D = 4096
HEADS = 32
KV_HEADS = 4
HEAD_DIM = 128
BLOCK = 64
LAYERS = 4
STEPS = 4
BLOCKS = 32
SEQ_LEN = 2048
QUERY_WIDTH = 4096
KV_WIDTH = 512
HEAD_BLOCKS = 4


def draw_block_table(key, part):
    half_count = BLOCKS // 2
    pair_order = jax.random.permutation(jax.random.fold_in(key, 1), half_count).astype(jnp.int32)
    flip_bits = jax.random.randint(jax.random.fold_in(key, 2), (half_count,), 0, 2)
    upper_block = BLOCKS - 1 - pair_order
    first_slot = jnp.where(flip_bits == 1, upper_block, pair_order)
    second_slot = jnp.where(flip_bits == 1, pair_order, upper_block)
    return jnp.stack([first_slot, second_slot], axis=1).reshape(BLOCKS).astype(jnp.int32)


def activation_rows(key, count):
    noise_draw = jax.random.normal(jax.random.fold_in(key, 1), (count, SEQ_LEN, D), jnp.float32)
    values = noise_draw
    return jnp.clip(values, -16.0, 16.0).astype(jnp.bfloat16)


def draw_hidden_in(key, part):
    return activation_rows(jax.random.fold_in(key, 11), LAYERS)


def draw_fresh_in(key, part):
    return activation_rows(jax.random.fold_in(key, 12), STEPS - 1)


def key_matrix(key):
    scale_value = D ** (-0.5)
    drawn = jax.random.normal(jax.random.fold_in(key, 101), (LAYERS, D, KV_HEADS * HEAD_DIM), jnp.float32)
    return jnp.clip(drawn, -6.0, 6.0) * scale_value


def draw_w_key(key, part):
    return key_matrix(key).astype(jnp.bfloat16)


def draw_w_query(key, part):
    scale_value = D ** (-0.5)
    noise_draw = jnp.clip(jax.random.normal(jax.random.fold_in(key, 102), (LAYERS, D, HEADS * HEAD_DIM), jnp.float32), -6.0, 6.0)
    values = 4.0 * scale_value * noise_draw
    return jnp.clip(values, -200.0 * scale_value, 200.0 * scale_value).astype(jnp.bfloat16)


def level_of(own_key, dims, split, low, high):
    factor_of = 1.0
    for position, parts in split:
        heights = jax.random.uniform(jax.random.fold_in(jax.random.fold_in(own_key, 6), position), (parts,), jnp.float32, low / len(split), high / len(split))
        factor_of = factor_of * jnp.repeat(jnp.exp(heights), dims[position] // parts).reshape((-1,) + (1,) * (len(dims) - 1 - position))
    return factor_of


def normal_values(key, dims, width, most, split=(), held_as=jnp.bfloat16):
    result = width * jax.random.normal(key, dims, jnp.float32)
    if split:
        result = result * level_of(key, dims, split, -0.22, 0.18)
    return jnp.clip(result, -most, most).astype(held_as)


def setup_inputs(seed: int = 0) -> dict:
    arg_keys = jax.random.split(jax.random.key(seed), 9)
    return {
        "hidden_in": draw_hidden_in(jax.random.fold_in(arg_keys[8], 71), 0),
        "fresh_in": draw_fresh_in(jax.random.fold_in(arg_keys[8], 71), 0),
        "block_table": draw_block_table(jax.random.fold_in(arg_keys[8], 71), 0),
        "norm_gain": jnp.clip(1.0 + 0.18 * jax.random.normal(arg_keys[3], (LAYERS, D), jnp.float32), 0.1, 1.9),
        "w_query": draw_w_query(jax.random.fold_in(arg_keys[8], 71), 0),
        "w_key": draw_w_key(jax.random.fold_in(arg_keys[8], 71), 0),
        "w_value": normal_values(arg_keys[6], (LAYERS, D, KV_WIDTH), D ** -0.5, 0.09375, ((0, 4), (1, 16), (2, 4))),
        "w_out": normal_values(arg_keys[7], (LAYERS, D, QUERY_WIDTH), QUERY_WIDTH ** -0.5, 0.09375, ((0, 4), (1, 16), (2, 4))),
    }


EPS = 1e-05
ROPE_BASE = 500000.0
NEGATIVE = -1e+30

def rotate(vectors, cosine_table, sine_table):
    half_width = vectors.shape[-1] // 2
    first_half = vectors[..., :half_width]
    second_half = vectors[..., half_width:]
    return jnp.concatenate([first_half * cosine_table - second_half * sine_table, second_half * cosine_table + first_half * sine_table], axis=-1)

def angle_tables(positions):
    half_width = HEAD_DIM // 2
    frequency = ROPE_BASE ** (-(jnp.arange(half_width, dtype=jnp.float32) * 2.0) / HEAD_DIM)
    angles = positions.astype(jnp.float32)[:, None] * frequency[None, :]
    return (jnp.cos(angles), jnp.sin(angles))

def apply_layer(current, gain_row, query_weights, key_weights, value_weights, output_weights, cosine_table, sine_table, allowed):
    score_scale = HEAD_DIM ** (-0.5)
    group_size = HEADS // KV_HEADS
    block_width = HEADS * HEAD_DIM // HEAD_BLOCKS
    widened = current.astype(jnp.float32)
    normed = (widened * lax.rsqrt(lax.optimization_barrier(jnp.mean(widened * widened, axis=-1, keepdims=True)) + EPS) * gain_row).astype(jnp.bfloat16)
    queries = jnp.dot(normed, query_weights, preferred_element_type=jnp.float32).reshape(SEQ_LEN, HEADS, HEAD_DIM)
    queries = rotate(queries, cosine_table, sine_table).astype(jnp.bfloat16)
    key_vecs = jnp.dot(normed, key_weights, preferred_element_type=jnp.float32).reshape(SEQ_LEN, KV_HEADS, HEAD_DIM)
    key_vecs = rotate(key_vecs, cosine_table, sine_table).astype(jnp.bfloat16)
    values = jnp.dot(normed, value_weights, preferred_element_type=jnp.float32).astype(jnp.bfloat16).reshape(SEQ_LEN, KV_HEADS, HEAD_DIM)
    query_heads = queries.transpose(1, 0, 2)
    key_heads = jnp.repeat(key_vecs, group_size, axis=1).transpose(1, 0, 2)
    value_heads = jnp.repeat(values, group_size, axis=1).transpose(1, 0, 2)

    def one_head(operands):
        query_head, key_head, value_head = operands
        scores = jnp.dot(query_head, key_head.T, preferred_element_type=jnp.float32) * score_scale
        largest = lax.optimization_barrier(jnp.max(jnp.where(allowed, scores, NEGATIVE), axis=-1, keepdims=True))
        weights = jnp.where(allowed, jnp.exp(scores - largest), 0.0)
        weight_sum = lax.optimization_barrier(jnp.sum(weights, axis=-1, keepdims=True))
        mixed = jnp.dot(weights.astype(jnp.bfloat16), value_head, preferred_element_type=jnp.float32)
        return (mixed / weight_sum).astype(jnp.bfloat16)
    attended = lax.map(one_head, (query_heads, key_heads, value_heads))
    attended = attended.transpose(1, 0, 2).reshape(SEQ_LEN, HEADS * HEAD_DIM)
    summed = jnp.zeros((SEQ_LEN, D), jnp.float32)
    for block_index in range(HEAD_BLOCKS):
        lower_col = block_index * block_width
        upper_col = lower_col + block_width
        partial_value = jnp.dot(attended[:, lower_col:upper_col], output_weights[:, lower_col:upper_col].T, preferred_element_type=jnp.float32)
        summed = summed + lax.optimization_barrier(partial_value.astype(jnp.bfloat16)).astype(jnp.float32)
    return (widened + summed).astype(jnp.bfloat16)

def reference(hidden_in, fresh_in, block_table, norm_gain, w_query, w_key, w_value, w_out):
    offsets = jnp.arange(BLOCK, dtype=jnp.int32)
    positions = (block_table.astype(jnp.int32)[:, None] * BLOCK + offsets[None, :]).reshape(SEQ_LEN).astype(jnp.int32)
    cosine_table, sine_table = angle_tables(positions)
    cosine_table = cosine_table[:, None, :]
    sine_table = sine_table[:, None, :]
    allowed = positions[None, :] <= positions[:, None]
    states = [hidden_in[layer_index] for layer_index in range(LAYERS)]
    all_steps = []
    for step_index in range(STEPS):
        produced = []
        for layer_index in range(LAYERS):
            produced.append(apply_layer(states[layer_index], norm_gain[layer_index], w_query[layer_index], w_key[layer_index], w_value[layer_index], w_out[layer_index], cosine_table, sine_table, allowed))
        all_steps.append(jnp.stack(produced))
        if step_index + 1 < STEPS:
            states = [fresh_in[step_index]] + produced[:-1]
    return jnp.stack(all_steps)
```

```python
import jax
import jax.numpy as jnp
from jax import lax
from jax.sharding import Mesh, PartitionSpec as P

HEAD_DIM = 128
BLOCK = 64


EPS = 1e-05
ROPE_BASE = 500000.0
NEGATIVE = -1e30
Z, XH, XL, CORE = 8, 2, 2, 2
PLANE = ("z", "xh", "xl", "core")


def moved(x, target):
    def flat(z, xh, xl, core):
        return ((z * XH + xh) * XL + xl) * CORE + core

    pairs = [
        (flat(z, xh, xl, core), flat(*target(z, xh, xl, core)))
        for z in range(Z)
        for xh in range(XH)
        for xl in range(XL)
        for core in range(CORE)
    ]
    return lax.ppermute(x, PLANE, pairs)


def swap_core(x):
    return moved(x, lambda z, xh, xl, core: (z, xh, xl, 1 - core))


def swap_x(x, dh, dl):
    return moved(x, lambda z, xh, xl, core: (z, xh ^ dh, xl ^ dl, core))


def from_z(x, by):
    return moved(x, lambda z, xh, xl, core: ((z - by) % Z, xh, xl, core))


def rotate(vectors, cosine_table, sine_table):
    half_width = vectors.shape[-1] // 2
    first_half = vectors[..., :half_width]
    second_half = vectors[..., half_width:]
    return jnp.concatenate(
        [
            first_half * cosine_table - second_half * sine_table,
            second_half * cosine_table + first_half * sine_table,
        ],
        axis=-1,
    )


def angle_tables(positions):
    half_width = HEAD_DIM // 2
    frequency = ROPE_BASE ** (-(jnp.arange(half_width, dtype=jnp.float32) * 2.0) / HEAD_DIM)
    angles = positions.astype(jnp.float32)[:, None] * frequency[None, :]
    return (jnp.cos(angles), jnp.sin(angles))


def row_positions(block_table, row_ids):
    slot_ids = row_ids // BLOCK
    matches = slot_ids[:, None] == jnp.arange(block_table.shape[0], dtype=jnp.int32)[None, :]
    owners = jnp.sum(jnp.where(matches, block_table[None, :], 0), axis=1)
    return owners * BLOCK + row_ids % BLOCK


def on_device(hidden_in, fresh_in, block_table, norm_gain, w_query, w_key, w_value, w_out):
    rows, wide = hidden_in.shape[1:]
    depth = w_query.shape[1]
    half = w_query.shape[2] // 2
    heads = half // HEAD_DIM
    sections = lax.axis_size("section")
    z, xh, xl, core = (lax.axis_index(name) for name in PLANE)
    tp = 2 * xl + core

    gain = lax.dynamic_slice_in_dim(norm_gain[0], (2 * z + xh) * depth, depth)[:, None]

    def spread(zero, one):
        first = moved(jnp.where(xh == 0, zero, one), lambda z, xh, xl, core: (z, xl, core, xh))
        second = moved(jnp.where(xh == 0, one, zero), lambda z, xh, xl, core: (z, xl, core, 1 - xh))
        both = jnp.where(
            core == 0,
            jnp.concatenate([first, second], axis=0),
            jnp.concatenate([second, first], axis=0),
        )
        return lax.all_gather(both, "z", axis=0, tiled=True)

    def own_order(w):
        return [lax.dynamic_slice_in_dim(w, (b ^ tp) * wide, wide) for b in range(4)]

    def scaled(wq, wkv):
        joined = jnp.concatenate([wq, wkv], axis=1).astype(jnp.float32) * gain
        return joined.astype(jnp.bfloat16)

    qkv_weights = spread(
        scaled(w_query[0][:, :half], w_key[0]), scaled(w_query[0][:, half:], w_value[0])
    )
    out_weights = spread(w_out[0][:, :half], w_out[0][:, half:])
    kv_weights = jnp.concatenate(own_order(qkv_weights[:, half:]), axis=0)
    query_weights = jnp.concatenate(own_order(qkv_weights[:, :half]), axis=0)
    out_blocks = own_order(out_weights)
    out_own = jnp.concatenate([out_blocks[0], out_blocks[2]], axis=0)
    out_other = jnp.concatenate([out_blocks[1], out_blocks[3]], axis=0)

    def plane_rows(plane):
        ids = jnp.arange(rows, dtype=jnp.int32)
        return jnp.concatenate(
            [(2 * plane + xh) * rows + ids, (2 * plane + (1 - xh)) * rows + ids]
        )

    positions = row_positions(block_table, plane_rows(z))
    key_positions = row_positions(
        block_table, jnp.concatenate([plane_rows((z + by) % Z) for by in range(Z)])
    )
    allowed = key_positions[None, :] <= positions[:, None]
    cosine_table, sine_table = angle_tables(positions)
    score_scale = HEAD_DIM ** (-0.5)
    query_cosine = (cosine_table * score_scale)[:, None, :]
    query_sine = (sine_table * score_scale)[:, None, :]
    kv_cosine = jnp.where(core == 0, cosine_table, 1.0)
    kv_sine = jnp.where(core == 0, sine_table, 0.0)
    last_section = lax.axis_index("section") == sections - 1
    ring = [(i, (i + 1) % sections) for i in range(sections)]

    produced = []
    current = hidden_in[0]
    for step_index in range(sections):
        near = swap_core(current)
        by_l, by_h, by_hl = swap_x(current, 0, 1), swap_x(current, 1, 0), swap_x(current, 1, 1)
        far_l, far_h, far_hl = swap_core(by_l), swap_core(by_h), swap_core(by_hl)
        full_rows = jnp.concatenate(
            [
                jnp.concatenate([current, near, by_l, far_l], axis=1),
                jnp.concatenate([by_h, far_h, by_hl, far_hl], axis=1),
            ],
            axis=0,
        )
        widened = full_rows.astype(jnp.float32)
        inverse = lax.rsqrt(jnp.mean(widened * widened, axis=-1, keepdims=True) + EPS)
        kv = jnp.dot(full_rows, kv_weights, preferred_element_type=jnp.float32) * inverse
        kv = rotate(kv, kv_cosine, kv_sine).astype(jnp.bfloat16)
        pieces = [kv] + [from_z(kv, by) for by in range(1, Z)]
        queries = jnp.dot(full_rows, query_weights, preferred_element_type=jnp.float32) * inverse
        queries = rotate(
            queries.reshape(2 * rows, heads, HEAD_DIM), query_cosine, query_sine
        ).astype(jnp.bfloat16)
        pair = lax.all_gather(jnp.concatenate(pieces, axis=0), "core", axis=0, tiled=False)
        scores = jnp.einsum("rgd,nd->grn", queries, pair[0], preferred_element_type=jnp.float32)
        largest = jnp.max(jnp.where(allowed, scores, NEGATIVE), axis=-1, keepdims=True)
        weights = jnp.where(allowed, jnp.exp(scores - largest), 0.0)
        weight_sum = jnp.sum(weights, axis=-1, keepdims=True)
        mixed = jnp.einsum(
            "grn,nd->grd",
            weights.astype(jnp.bfloat16),
            pair[1],
            preferred_element_type=jnp.float32,
        )
        attended = (mixed / weight_sum).astype(jnp.bfloat16)
        attended = attended.transpose(1, 0, 2).reshape(2 * rows, half)

        def project(w):
            return lax.dot_general(
                attended, w, (((1,), (1,)), ((), ())), preferred_element_type=jnp.float32
            )

        arrived = swap_core(project(out_other).astype(jnp.bfloat16))
        paired = project(out_own) + arrived.astype(jnp.float32)
        own = paired[:rows, :wide]
        sent = paired.astype(jnp.bfloat16)
        from_l = swap_x(sent[:rows, wide:], 0, 1)
        from_h = swap_x(sent[rows:, :wide], 1, 0)
        from_hl = swap_x(sent[rows:, wide:], 1, 1)
        summed = (own + from_l.astype(jnp.float32)) + (
            from_h.astype(jnp.float32) + from_hl.astype(jnp.float32)
        )
        result = (current.astype(jnp.float32) + summed).astype(jnp.bfloat16)
        produced.append(result)
        if step_index + 1 < sections:
            onward = jnp.where(last_section, fresh_in[step_index], result)
            current = lax.ppermute(onward, "section", ring)
    return jnp.stack(produced)[:, None]


def solution(mesh):
    split = Mesh(
        mesh.devices.reshape(mesh.devices.shape[0], Z, XH, XL, CORE), ("section",) + PLANE
    )
    rows, columns = ("z", "xh"), ("xl", "core")
    in_specs = (
        P("section", rows, columns),
        P(None, rows, columns),
        P(),
        P("section", None),
        P("section", rows, columns),
        P("section", rows, columns),
        P("section", rows, columns),
        P("section", rows, columns),
    )
    out_specs = P(None, "section", rows, columns)
    return jax.shard_map(
        on_device, mesh=split, in_specs=in_specs, out_specs=out_specs, check_vma=False
    )
```

```python
import jax
import jax.numpy as jnp
from jax import lax
from jax.experimental import pallas as pl
from jax.experimental.pallas import tpu as pltpu
from jax.sharding import Mesh, PartitionSpec as P

HEAD_DIM = 128
BLOCK = 64


EPS = 1e-05
ROPE_BASE = 500000.0
NEGATIVE = -1e30
LOG2_E = 1.4426950408889634
Z, XH, XL, CORE = 8, 2, 2, 2
PLANE = ("z", "xh", "xl", "core")


def moved(x, target):
    def flat(z, xh, xl, core):
        return ((z * XH + xh) * XL + xl) * CORE + core

    pairs = [
        (flat(z, xh, xl, core), flat(*target(z, xh, xl, core)))
        for z in range(Z)
        for xh in range(XH)
        for xl in range(XL)
        for core in range(CORE)
    ]
    return lax.ppermute(x, PLANE, pairs)


def swap_core(x):
    return moved(x, lambda z, xh, xl, core: (z, xh, xl, 1 - core))


def swap_x(x, dh, dl):
    return moved(x, lambda z, xh, xl, core: (z, xh ^ dh, xl ^ dl, core))


def from_z(x, by):
    return moved(x, lambda z, xh, xl, core: ((z - (1 - 2 * core) * by) % Z, xh, xl, core))


WHOLE = pl.BlockSpec(memory_space=pltpu.VMEM)


def turned(x, cosine, sine):
    return x * cosine + pltpu.roll(x, x.shape[-1] // 2, 1) * sine


def kv_kernel(count, tp_ref, *refs):
    pieces, (w_ref, cosine_ref, sine_ref, kv_ref, inverse_ref, total, squares) = refs[:8], refs[8:]
    j = pl.program_id(0)

    @pl.when(j == 0)
    def _():
        total[...] = jnp.zeros_like(total)
        squares[...] = jnp.zeros_like(squares)

    for k in range(4):

        @pl.when(j == k)
        def _():
            x = jnp.concatenate([pieces[k][...], pieces[4 + k][...]], axis=0)
            total[...] += jnp.dot(x, w_ref[...], preferred_element_type=jnp.float32)
            wide = x.astype(jnp.float32)
            lanes = squares.shape[1]
            part = squares[...]
            for c in range(x.shape[1] // lanes):
                chunk = wide[:, c * lanes : (c + 1) * lanes]
                part += chunk * chunk
            squares[...] = part

    @pl.when(j == 3)
    def _():
        mean = jnp.sum(squares[...], axis=1, keepdims=True) * (1.0 / count)
        inverse = jnp.broadcast_to(lax.rsqrt(mean + EPS), inverse_ref.shape)
        inverse_ref[...] = inverse
        kv = turned(total[...] * inverse, cosine_ref[...], sine_ref[...])
        kv_ref[...] = kv.astype(kv_ref.dtype)


def query_kernel(tp_ref, *refs):
    pieces, (w_ref, cosine_ref, sine_ref, inverse_ref, query_ref, total) = refs[:8], refs[8:]
    j = pl.program_id(0)

    for k in range(4):

        @pl.when(j == k)
        def _():
            x = jnp.concatenate([pieces[k][...], pieces[4 + k][...]], axis=0)
            part = jnp.dot(x, w_ref[...], preferred_element_type=jnp.float32)
            total[...] = part if k == 0 else total[...] + part

    @pl.when(j == 3)
    def _():
        for h in range(total.shape[1] // HEAD_DIM):
            cut = slice(h * HEAD_DIM, (h + 1) * HEAD_DIM)
            head = total[:, cut] * inverse_ref[...]
            query_ref[:, cut] = turned(head, cosine_ref[...], sine_ref[...]).astype(query_ref.dtype)


def project_kv(tp, pieces, weights, cosine, sine):
    rows, wide = pieces[0].shape
    width = HEAD_DIM
    column = weights.shape[1] // width - 1
    return pl.pallas_call(
        lambda *refs: kv_kernel(4 * wide, *refs),
        out_shape=(
            jax.ShapeDtypeStruct((2 * rows, width), jnp.bfloat16),
            jax.ShapeDtypeStruct((2 * rows, width), jnp.float32),
        ),
        grid_spec=pltpu.PrefetchScalarGridSpec(
            num_scalar_prefetch=1,
            grid=(4,),
            in_specs=[WHOLE] * 8
            + [pl.BlockSpec((wide, width), lambda j, tp: (j ^ tp[0], column))]
            + [WHOLE] * 2,
            out_specs=(WHOLE, WHOLE),
            scratch_shapes=[pltpu.VMEM((2 * rows, width), jnp.float32)] * 2,
        ),
        cost_estimate=pl.CostEstimate(
            flops=16 * rows * wide * width,
            bytes_accessed=8 * wide * (rows * 2 + width),
            transcendentals=0,
        ),
        name="project_kv",
    )(tp, *pieces, weights, cosine, sine)


def project_query(tp, pieces, weights, cosine, sine, inverse):
    rows, wide = pieces[0].shape
    width = weights.shape[1] - HEAD_DIM
    return pl.pallas_call(
        query_kernel,
        out_shape=jax.ShapeDtypeStruct((2 * rows, width), jnp.bfloat16),
        grid_spec=pltpu.PrefetchScalarGridSpec(
            num_scalar_prefetch=1,
            grid=(4,),
            in_specs=[WHOLE] * 8
            + [pl.BlockSpec((wide, width), lambda j, tp: (j ^ tp[0], 0))]
            + [WHOLE] * 3,
            out_specs=WHOLE,
            scratch_shapes=[pltpu.VMEM((2 * rows, width), jnp.float32)],
        ),
        cost_estimate=pl.CostEstimate(
            flops=16 * rows * wide * width,
            bytes_accessed=8 * wide * (rows * 2 + width),
            transcendentals=0,
        ),
        name="project_query",
    )(tp, *pieces, weights, cosine, sine, inverse)


def attention_kernel(core_ref, q_ref, qpos_ref, kpos_ref, *refs):
    blocks, halves, (out_ref, scores) = refs[:7], refs[7:9], refs[9:]
    span = blocks[0].shape[0]
    first_core = core_ref[0] == 0
    mine, other = halves[0][...], halves[1][...]
    keys = [b[:, :HEAD_DIM] for b in blocks] + [jnp.where(first_core, mine, other)]
    values = [b[:, HEAD_DIM:] for b in blocks] + [jnp.where(first_core, other, mine)]
    qpos = qpos_ref[...]
    for h in range(q_ref.shape[1] // HEAD_DIM):
        cut = slice(h * HEAD_DIM, (h + 1) * HEAD_DIM)
        q = q_ref[:, cut]
        top = None
        for b, key in enumerate(keys):
            s = lax.dot_general(
                q, key, (((1,), (1,)), ((), ())), preferred_element_type=jnp.float32
            )
            s = jnp.where(kpos_ref[:, b * span : (b + 1) * span] <= qpos, s, NEGATIVE)
            scores[:, b * span : (b + 1) * span] = s
            top = s if top is None else jnp.maximum(top, s)
        top = jnp.max(top, axis=1, keepdims=True)
        mixed, total = None, None
        for b, value in enumerate(values):
            p = jnp.exp2(scores[:, b * span : (b + 1) * span] - top)
            part = jnp.dot(p.astype(value.dtype), value, preferred_element_type=jnp.float32)
            mixed = part if mixed is None else mixed + part
            total = p if total is None else total + p
        weight_sum = jnp.sum(total, axis=1, keepdims=True)
        out_ref[:, cut] = (mixed / weight_sum).astype(out_ref.dtype)


def attend(core, queries, qpos, kpos, blocks, halves):
    rows, width = queries.shape
    span = kpos.shape[1]
    return pl.pallas_call(
        attention_kernel,
        out_shape=jax.ShapeDtypeStruct(queries.shape, jnp.bfloat16),
        in_specs=[pl.BlockSpec(memory_space=pltpu.SMEM)] + [WHOLE] * (3 + 7 + 2),
        out_specs=WHOLE,
        scratch_shapes=[pltpu.VMEM((rows, span), jnp.float32)],
        cost_estimate=pl.CostEstimate(
            flops=4 * rows * width * span,
            bytes_accessed=4 * rows * width + 4 * span * HEAD_DIM,
            transcendentals=rows * width // HEAD_DIM * span,
        ),
        name="attend",
    )(core, queries, qpos, kpos, *blocks, *halves)


def angle_tables(positions):
    half_width = HEAD_DIM // 2
    frequency = ROPE_BASE ** (-(jnp.arange(half_width, dtype=jnp.float32) * 2.0) / HEAD_DIM)
    angles = positions.astype(jnp.float32)[:, None] * frequency[None, :]
    return (jnp.cos(angles), jnp.sin(angles))


def row_positions(block_table, row_ids):
    slot_ids = row_ids // BLOCK
    matches = slot_ids[:, None] == jnp.arange(block_table.shape[0], dtype=jnp.int32)[None, :]
    owners = jnp.sum(jnp.where(matches, block_table[None, :], 0), axis=1)
    return owners * BLOCK + row_ids % BLOCK


def on_device(hidden_in, fresh_in, block_table, norm_gain, w_query, w_key, w_value, w_out):
    rows, wide = hidden_in.shape[1:]
    depth = w_query.shape[1]
    half = w_query.shape[2] // 2
    sections = lax.axis_size("section")
    z, xh, xl, core = (lax.axis_index(name) for name in PLANE)
    tp = 2 * xl + core

    gain = lax.dynamic_slice_in_dim(norm_gain[0], (2 * z + xh) * depth, depth)[:, None]

    def exchanged(zero, one):
        first = moved(jnp.where(xh == 0, zero, one), lambda z, xh, xl, core: (z, xl, core, xh))
        second = moved(jnp.where(xh == 0, one, zero), lambda z, xh, xl, core: (z, xl, core, 1 - xh))
        return jnp.where(
            core == 0,
            jnp.concatenate([first, second], axis=0),
            jnp.concatenate([second, first], axis=0),
        )

    def scaled(wq, wkv):
        joined = jnp.concatenate([wq, wkv], axis=1).astype(jnp.float32) * gain
        return joined.astype(jnp.bfloat16)

    qkv_block = exchanged(
        scaled(w_query[0][:, :half], w_key[0]), scaled(w_query[0][:, half:], w_value[0])
    )
    qkv_block, out_source = lax.optimization_barrier((qkv_block, w_out[0]))
    qkv_weights = lax.all_gather(qkv_block, "z", axis=0, tiled=True)
    out_block = exchanged(out_source[:, :half], out_source[:, half:])
    out_weights = lax.all_gather(out_block, "z", axis=0, tiled=True)
    out_blocks = [lax.dynamic_slice_in_dim(out_weights, (b ^ tp) * wide, wide) for b in range(4)]
    out_own = jnp.concatenate([out_blocks[0], out_blocks[2]], axis=0)
    out_other = jnp.concatenate([out_blocks[1], out_blocks[3]], axis=0)

    def plane_rows(plane):
        ids = jnp.arange(rows, dtype=jnp.int32)
        return jnp.concatenate(
            [(2 * plane + xh) * rows + ids, (2 * plane + (1 - xh)) * rows + ids]
        )

    positions = row_positions(block_table, plane_rows(z))
    toward = 1 - 2 * core
    steps = [0, toward, 2 * toward, 3 * toward, -toward, -2 * toward, -3 * toward, 4]
    key_positions = row_positions(
        block_table, jnp.concatenate([plane_rows((z + by + Z) % Z) for by in steps])
    )
    query_positions, key_positions = positions[:, None], key_positions[None, :]
    cosine_table, sine_table = angle_tables(positions)
    cosine_table = jnp.concatenate([cosine_table, cosine_table], axis=1)
    sine_table = jnp.concatenate([-sine_table, sine_table], axis=1)
    score_scale = HEAD_DIM ** (-0.5) * LOG2_E
    query_cosine, query_sine = cosine_table * score_scale, sine_table * score_scale
    kv_cosine = jnp.where(core == 0, cosine_table, 1.0)
    kv_sine = jnp.where(core == 0, sine_table, 0.0)
    tp_scalar = tp.astype(jnp.int32).reshape(1)
    core_scalar = core.astype(jnp.int32).reshape(1)
    last_section = lax.axis_index("section") == sections - 1
    ring = [(i, (i + 1) % sections) for i in range(sections)]

    produced = []
    current = hidden_in[0]
    for step_index in range(sections):
        near = swap_core(current)
        by_l, by_h, by_hl = swap_x(current, 0, 1), swap_x(current, 1, 0), swap_x(current, 1, 1)
        far_l, far_h, far_hl = swap_core(by_l), swap_core(by_h), swap_core(by_hl)
        x = [current, near, by_l, far_l, by_h, far_h, by_hl, far_hl]
        kv, inverse = project_kv(tp_scalar, x, qkv_weights, kv_cosine, kv_sine)
        opposite = moved(kv, lambda z, xh, xl, core: ((z + Z // 2) % Z, xh, xl, core))
        partner = swap_core(kv)
        own_block = jnp.where(
            core == 0,
            jnp.concatenate([kv, partner], axis=1),
            jnp.concatenate([partner, kv], axis=1),
        )
        fetched = [from_z(own_block, by) for by in (1, 2, 3)]
        queries = project_query(tp_scalar, x, qkv_weights, query_cosine, query_sine, inverse)
        blocks = [own_block] + fetched + [swap_core(block) for block in fetched]
        halves = [opposite, swap_core(opposite)]
        attended = attend(core_scalar, queries, query_positions, key_positions, blocks, halves)

        def project(w):
            return lax.dot_general(
                attended, w, (((1,), (1,)), ((), ())), preferred_element_type=jnp.float32
            )

        arrived = swap_core(project(out_other).astype(jnp.bfloat16))
        paired = project(out_own) + arrived.astype(jnp.float32)
        own = paired[:rows, :wide]
        sent = paired.astype(jnp.bfloat16)
        from_l = swap_x(sent[:rows, wide:], 0, 1)
        from_h = swap_x(sent[rows:, :wide], 1, 0)
        from_hl = swap_x(sent[rows:, wide:], 1, 1)
        summed = (own + from_l.astype(jnp.float32)) + (
            from_h.astype(jnp.float32) + from_hl.astype(jnp.float32)
        )
        result = (current.astype(jnp.float32) + summed).astype(jnp.bfloat16)
        produced.append(result)
        if step_index + 1 < sections:
            onward = jnp.where(last_section, fresh_in[step_index], result)
            current = lax.ppermute(onward, "section", ring)
    return jnp.stack(produced)[:, None]


def solution(mesh):
    split = Mesh(
        mesh.devices.reshape(mesh.devices.shape[0], Z, XH, XL, CORE), ("section",) + PLANE
    )
    rows, columns = ("z", "xh"), ("xl", "core")
    in_specs = (
        P("section", rows, columns),
        P(None, rows, columns),
        P(),
        P("section", None),
        P("section", rows, columns),
        P("section", rows, columns),
        P("section", rows, columns),
        P("section", rows, columns),
    )
    out_specs = P(None, "section", rows, columns)
    return jax.shard_map(
        on_device, mesh=split, in_specs=in_specs, out_specs=out_specs, check_vma=False
    )
```

```python
import functools

import jax
import jax.numpy as jnp
from jax import lax
from jax.experimental import pallas as pl
from jax.experimental.pallas import tpu as pltpu
from jax.sharding import Mesh, PartitionSpec as P


HEAD_DIM = 128
BLOCK = 64


EPS = 1e-05
ROPE_BASE = 500000.0
NEGATIVE = -1e30
LOG2_E = 1.4426950408889634
Z, XH, XL, CORE = 8, 2, 2, 2
PLANE = ("z", "xh", "xl", "core")


def moved(x, target):
    def flat(z, xh, xl, core):
        return ((z * XH + xh) * XL + xl) * CORE + core

    pairs = [
        (flat(z, xh, xl, core), flat(*target(z, xh, xl, core)))
        for z in range(Z)
        for xh in range(XH)
        for xl in range(XL)
        for core in range(CORE)
    ]
    return lax.ppermute(x, PLANE, pairs)


def swap_core(x):
    return moved(x, lambda z, xh, xl, core: (z, xh, xl, 1 - core))


def swap_x(x, dh, dl):
    return moved(x, lambda z, xh, xl, core: (z, xh ^ dh, xl ^ dl, core))


def from_z(x, by):
    return moved(x, lambda z, xh, xl, core: ((z - (1 - 2 * core) * by) % Z, xh, xl, core))


WHOLE = pl.BlockSpec(memory_space=pltpu.VMEM)


def turned(x, cosine, sine):
    return x * cosine + pltpu.roll(x, x.shape[-1] // 2, 1) * sine


def weight_copies(tp_ref, w_ref, held, sems, column, order):
    wide, width = held.shape[1:]
    copies = []
    for place, partner in enumerate(order):
        first = pl.multiple_of((tp_ref[0] ^ partner) * wide, wide)
        block = w_ref.at[pl.ds(first, wide), pl.ds(column, width)]
        copies.append(pltpu.make_async_copy(block, held.at[place], sems.at[place]))
    for copy in copies:
        copy.start()
    return copies


def kv_kernel(tp_ref, *refs):
    pieces, (w_ref, cosine_ref, sine_ref, kv_ref, inverse_ref, held, sems) = refs[:8], refs[8:]
    rows, wide = pieces[0].shape
    width = held.shape[2]
    copies = weight_copies(tp_ref, w_ref, held, sems, w_ref.shape[1] - width, range(4))
    total = jnp.zeros((2 * rows, width), jnp.float32)
    squares = jnp.zeros((2 * rows, width), jnp.float32)
    for k in range(4):
        for c in range(wide // width):
            cut = slice(c * width, (c + 1) * width)
            chunk = jnp.concatenate([pieces[k][:, cut], pieces[4 + k][:, cut]], axis=0)
            chunk = chunk.astype(jnp.float32)
            squares += chunk * chunk
    for k in range(4):
        copies[k].wait()
        x = jnp.concatenate([pieces[k][...], pieces[4 + k][...]], axis=0)
        total += jnp.dot(x, held[k], preferred_element_type=jnp.float32)
    mean = jnp.sum(squares, axis=1, keepdims=True) * (1.0 / (4 * wide))
    inverse = jnp.broadcast_to(lax.rsqrt(mean + EPS), inverse_ref.shape)
    inverse_ref[...] = inverse
    kv_ref[...] = turned(total * inverse, cosine_ref[...], sine_ref[...]).astype(kv_ref.dtype)


def query_kernel(tp_ref, *refs):
    pieces, (w_ref, cosine_ref, sine_ref, inverse_ref, query_ref, total, held, sems) = (
        refs[:8],
        refs[8:],
    )
    copies = weight_copies(tp_ref, w_ref, held, sems, 0, range(4))
    for k in range(4):
        copies[k].wait()
        x = jnp.concatenate([pieces[k][...], pieces[4 + k][...]], axis=0)
        part = jnp.dot(x, held[k], preferred_element_type=jnp.float32)
        total[...] = part if k == 0 else total[...] + part
    for h in range(total.shape[1] // HEAD_DIM):
        cut = slice(h * HEAD_DIM, (h + 1) * HEAD_DIM)
        head = total[:, cut] * inverse_ref[...]
        query_ref[:, cut] = turned(head, cosine_ref[...], sine_ref[...]).astype(query_ref.dtype)


SCALAR = pl.BlockSpec(memory_space=pltpu.SMEM)
FAR = pl.BlockSpec(memory_space=pltpu.HBM)


def project_kv(tp, pieces, weights, cosine, sine):
    rows, wide = pieces[0].shape
    width = HEAD_DIM
    return pl.pallas_call(
        kv_kernel,
        out_shape=(
            jax.ShapeDtypeStruct((2 * rows, width), jnp.bfloat16),
            jax.ShapeDtypeStruct((2 * rows, width), jnp.float32),
        ),
        in_specs=[SCALAR] + [WHOLE] * 8 + [FAR] + [WHOLE] * 2,
        out_specs=(WHOLE, WHOLE),
        scratch_shapes=[
            pltpu.VMEM((4, wide, width), jnp.bfloat16),
            pltpu.SemaphoreType.DMA((4,)),
        ],
        cost_estimate=pl.CostEstimate(
            flops=16 * rows * wide * width,
            bytes_accessed=8 * wide * (rows * 2 + width),
            transcendentals=0,
        ),
        compiler_params=pltpu.CompilerParams(vmem_limit_bytes=8 << 20),
        name="project_kv",
    )(tp, *pieces, weights, cosine, sine)


def project_query(tp, pieces, weights, cosine, sine, inverse):
    rows, wide = pieces[0].shape
    width = weights.shape[1] - HEAD_DIM
    return pl.pallas_call(
        query_kernel,
        out_shape=jax.ShapeDtypeStruct((2 * rows, width), jnp.bfloat16),
        in_specs=[SCALAR] + [WHOLE] * 8 + [FAR] + [WHOLE] * 3,
        out_specs=WHOLE,
        scratch_shapes=[
            pltpu.VMEM((2 * rows, width), jnp.float32),
            pltpu.VMEM((4, wide, width), jnp.bfloat16),
            pltpu.SemaphoreType.DMA((4,)),
        ],
        cost_estimate=pl.CostEstimate(
            flops=16 * rows * wide * width,
            bytes_accessed=8 * wide * (rows * 2 + width),
            transcendentals=0,
        ),
        compiler_params=pltpu.CompilerParams(vmem_limit_bytes=12 << 20),
        name="project_query",
    )(tp, *pieces, weights, cosine, sine, inverse)


def attention_kernel(core_ref, q_ref, qpos_ref, kpos_ref, *refs):
    blocks, halves, (out_ref, scores) = refs[:7], refs[7:9], refs[9:]
    span = blocks[0].shape[0]
    first_core = core_ref[0] == 0
    mine, other = halves[0][...], halves[1][...]
    keys = [b[:, :HEAD_DIM] for b in blocks] + [jnp.where(first_core, mine, other)]
    values = [b[:, HEAD_DIM:] for b in blocks] + [jnp.where(first_core, other, mine)]
    qpos = qpos_ref[...]

    def one_head(h, carry):
        cut = pl.ds(pl.multiple_of(h * HEAD_DIM, HEAD_DIM), HEAD_DIM)
        q = q_ref[:, cut]
        top = None
        for b, key in enumerate(keys):
            s = lax.dot_general(
                q, key, (((1,), (1,)), ((), ())), preferred_element_type=jnp.float32
            )
            s = jnp.where(kpos_ref[:, b * span : (b + 1) * span] <= qpos, s, NEGATIVE)
            scores[:, b * span : (b + 1) * span] = s
            top = s if top is None else jnp.maximum(top, s)
        top = jnp.max(top, axis=1, keepdims=True)
        mixed, total = None, None
        for b, value in enumerate(values):
            p = jnp.exp2(scores[:, b * span : (b + 1) * span] - top)
            part = jnp.dot(p.astype(value.dtype), value, preferred_element_type=jnp.float32)
            mixed = part if mixed is None else mixed + part
            total = p if total is None else total + p
        weight_sum = jnp.sum(total, axis=1, keepdims=True)
        out_ref[:, cut] = (mixed / weight_sum).astype(out_ref.dtype)
        return carry

    lax.fori_loop(0, q_ref.shape[1] // HEAD_DIM, one_head, 0)


def attend(core, queries, qpos, kpos, blocks, halves):
    rows, width = queries.shape
    span = kpos.shape[1]
    return pl.pallas_call(
        attention_kernel,
        out_shape=jax.ShapeDtypeStruct(queries.shape, jnp.bfloat16),
        in_specs=[SCALAR] + [WHOLE] * (3 + 7 + 2),
        out_specs=WHOLE,
        scratch_shapes=[pltpu.VMEM((rows, span), jnp.float32)],
        cost_estimate=pl.CostEstimate(
            flops=4 * rows * width * span,
            bytes_accessed=4 * rows * width + 4 * span * HEAD_DIM,
            transcendentals=rows * width // HEAD_DIM * span,
        ),
        compiler_params=pltpu.CompilerParams(vmem_limit_bytes=12 << 20),
        name="attend",
    )(core, queries, qpos, kpos, *blocks, *halves)


def out_kernel(odd, tp_ref, attended_ref, w_ref, out_ref, held, sems):
    wide = held.shape[1]
    copies = weight_copies(tp_ref, w_ref, held, sems, 0, (odd, 2 + odd))
    for place in range(2):
        copies[place].wait()
        part = lax.dot_general(
            attended_ref[...],
            held[place],
            (((1,), (1,)), ((), ())),
            preferred_element_type=jnp.float32,
        )
        out_ref[:, place * wide : (place + 1) * wide] = part.astype(out_ref.dtype)


def project_out(tp, attended, weights, wide, odd):
    rows, half = attended.shape
    return pl.pallas_call(
        functools.partial(out_kernel, odd),
        out_shape=jax.ShapeDtypeStruct((rows, 2 * wide), jnp.bfloat16),
        in_specs=[SCALAR, WHOLE, FAR],
        out_specs=WHOLE,
        scratch_shapes=[
            pltpu.VMEM((2, wide, half), jnp.bfloat16),
            pltpu.SemaphoreType.DMA((2,)),
        ],
        cost_estimate=pl.CostEstimate(
            flops=4 * rows * wide * half,
            bytes_accessed=4 * wide * half + 4 * wide * rows + 2 * rows * half,
            transcendentals=0,
        ),
        compiler_params=pltpu.CompilerParams(vmem_limit_bytes=8 << 20),
        name="project_out",
    )(tp, attended, weights)


def angle_tables(positions):
    half_width = HEAD_DIM // 2
    frequency = ROPE_BASE ** (-(jnp.arange(half_width, dtype=jnp.float32) * 2.0) / HEAD_DIM)
    angles = positions.astype(jnp.float32)[:, None] * frequency[None, :]
    return (jnp.cos(angles), jnp.sin(angles))


def row_positions(block_table, row_ids):
    slot_ids = row_ids // BLOCK
    matches = slot_ids[:, None] == jnp.arange(block_table.shape[0], dtype=jnp.int32)[None, :]
    owners = jnp.sum(jnp.where(matches, block_table[None, :], 0), axis=1)
    return owners * BLOCK + row_ids % BLOCK


def on_device(hidden_in, fresh_in, block_table, norm_gain, w_query, w_key, w_value, w_out):
    rows, wide = hidden_in.shape[1:]
    depth = w_query.shape[1]
    half = w_query.shape[2] // 2
    sections = lax.axis_size("section")
    z, xh, xl, core = (lax.axis_index(name) for name in PLANE)
    tp = 2 * xl + core

    gain = lax.dynamic_slice_in_dim(norm_gain[0], (2 * z + xh) * depth, depth)[:, None]

    def exchanged(zero, one):
        first = moved(jnp.where(xh == 0, zero, one), lambda z, xh, xl, core: (z, xl, core, xh))
        second = moved(jnp.where(xh == 0, one, zero), lambda z, xh, xl, core: (z, xl, core, 1 - xh))
        return jnp.where(
            core == 0,
            jnp.concatenate([first, second], axis=0),
            jnp.concatenate([second, first], axis=0),
        )

    def scaled(wq, wkv):
        joined = jnp.concatenate([wq, wkv], axis=1).astype(jnp.float32) * gain
        return joined.astype(jnp.bfloat16)

    qkv_block = exchanged(
        scaled(w_query[0][:, :half], w_key[0]), scaled(w_query[0][:, half:], w_value[0])
    )
    qkv_block, out_source = lax.optimization_barrier((qkv_block, w_out[0]))
    qkv_weights = lax.all_gather(qkv_block, "z", axis=0, tiled=True)
    out_block = exchanged(out_source[:, :half], out_source[:, half:])
    out_weights = lax.all_gather(out_block, "z", axis=0, tiled=True)

    def plane_rows(plane):
        ids = jnp.arange(rows, dtype=jnp.int32)
        return jnp.concatenate(
            [(2 * plane + xh) * rows + ids, (2 * plane + (1 - xh)) * rows + ids]
        )

    positions = row_positions(block_table, plane_rows(z))
    toward = 1 - 2 * core
    steps = [0, toward, 2 * toward, 3 * toward, -toward, -2 * toward, -3 * toward, 4]
    key_positions = row_positions(
        block_table, jnp.concatenate([plane_rows((z + by + Z) % Z) for by in steps])
    )
    query_positions, key_positions = positions[:, None], key_positions[None, :]
    cosine_table, sine_table = angle_tables(positions)
    cosine_table = jnp.concatenate([cosine_table, cosine_table], axis=1)
    sine_table = jnp.concatenate([-sine_table, sine_table], axis=1)
    score_scale = HEAD_DIM ** (-0.5) * LOG2_E
    query_cosine, query_sine = cosine_table * score_scale, sine_table * score_scale
    kv_cosine = jnp.where(core == 0, cosine_table, 1.0)
    kv_sine = jnp.where(core == 0, sine_table, 0.0)
    tp_scalar = tp.astype(jnp.int32).reshape(1)
    core_scalar = core.astype(jnp.int32).reshape(1)
    last_section = lax.axis_index("section") == sections - 1
    ring = [(i, (i + 1) % sections) for i in range(sections)]

    produced = []
    current = hidden_in[0]
    for step_index in range(sections):
        near = swap_core(current)
        by_l, by_h, by_hl = swap_x(current, 0, 1), swap_x(current, 1, 0), swap_x(current, 1, 1)
        far_l, far_h, far_hl = swap_core(by_l), swap_core(by_h), swap_core(by_hl)
        x = [current, near, by_l, far_l, by_h, far_h, by_hl, far_hl]
        kv, inverse = project_kv(tp_scalar, x, qkv_weights, kv_cosine, kv_sine)
        opposite = moved(kv, lambda z, xh, xl, core: ((z + Z // 2) % Z, xh, xl, core))
        partner = swap_core(kv)
        own_block = jnp.where(
            core == 0,
            jnp.concatenate([kv, partner], axis=1),
            jnp.concatenate([partner, kv], axis=1),
        )
        fetched = []
        for by in (1, 2, 3):
            fetched.append(from_z(own_block, by))
        queries = project_query(tp_scalar, x, qkv_weights, query_cosine, query_sine, inverse)
        blocks = [own_block] + fetched + [swap_core(block) for block in fetched]
        halves = [opposite, swap_core(opposite)]
        attended = attend(
            core_scalar, queries, query_positions, key_positions, blocks, halves
        )
        leaving = project_out(tp_scalar, attended, out_weights, wide, 1)
        arrived = swap_core(leaving)
        staying = project_out(tp_scalar, attended, out_weights, wide, 0)
        paired = staying.astype(jnp.float32) + arrived.astype(jnp.float32)
        own = paired[:rows, :wide]
        sent = paired.astype(jnp.bfloat16)
        from_l = swap_x(sent[:rows, wide:], 0, 1)
        from_h = swap_x(sent[rows:, :wide], 1, 0)
        from_hl = swap_x(sent[rows:, wide:], 1, 1)
        summed = (own + from_l.astype(jnp.float32)) + (
            from_h.astype(jnp.float32) + from_hl.astype(jnp.float32)
        )
        result = (current.astype(jnp.float32) + summed).astype(jnp.bfloat16)
        produced.append(result)
        if step_index + 1 < sections:
            onward = jnp.where(last_section, fresh_in[step_index], result)
            current = lax.ppermute(onward, "section", ring)
    return jnp.stack(produced)[:, None]


def solution(mesh):
    split = Mesh(
        mesh.devices.reshape(mesh.devices.shape[0], Z, XH, XL, CORE), ("section",) + PLANE
    )
    rows, columns = ("z", "xh"), ("xl", "core")
    in_specs = (
        P("section", rows, columns),
        P(None, rows, columns),
        P(),
        P("section", None),
        P("section", rows, columns),
        P("section", rows, columns),
        P("section", rows, columns),
        P("section", rows, columns),
    )
    out_specs = P(None, "section", rows, columns)
    return jax.shard_map(
        on_device, mesh=split, in_specs=in_specs, out_specs=out_specs, check_vma=False
    )
```

```python
import functools

import jax
import jax.numpy as jnp
from jax import lax
from jax.experimental import pallas as pl
from jax.experimental.pallas import tpu as pltpu
from jax.sharding import Mesh, PartitionSpec as P


HEAD_DIM = 128
BLOCK = 64


EPS = 1e-05
ROPE_BASE = 500000.0
NEGATIVE = -1e30
LOG2_E = 1.4426950408889634
Z, XH, XL, CORE = 8, 2, 2, 2
PLANE = ("z", "xh", "xl", "core")


def moved(x, target):
    def flat(z, xh, xl, core):
        return ((z * XH + xh) * XL + xl) * CORE + core

    pairs = [
        (flat(z, xh, xl, core), flat(*target(z, xh, xl, core)))
        for z in range(Z)
        for xh in range(XH)
        for xl in range(XL)
        for core in range(CORE)
    ]
    return lax.ppermute(x, PLANE, pairs)


def swap_core(x):
    return moved(x, lambda z, xh, xl, core: (z, xh, xl, 1 - core))


def swap_x(x, dh, dl):
    return moved(x, lambda z, xh, xl, core: (z, xh ^ dh, xl ^ dl, core))


def from_z(x, by):
    return moved(x, lambda z, xh, xl, core: ((z - (1 - 2 * core) * by) % Z, xh, xl, core))


WHOLE = pl.BlockSpec(memory_space=pltpu.VMEM)


def turned(x, cosine, sine):
    return x * cosine + pltpu.roll(x, x.shape[-1] // 2, 1) * sine


def weight_copies(tp_ref, w_ref, held, sems, column, order):
    wide, width = held.shape[1:]
    copies = []
    for place, partner in enumerate(order):
        first = pl.multiple_of((tp_ref[0] ^ partner) * wide, wide)
        block = w_ref.at[pl.ds(first, wide), pl.ds(column, width)]
        copies.append(pltpu.make_async_copy(block, held.at[place], sems.at[place]))
    for copy in copies:
        copy.start()
    return copies


def kv_kernel(tp_ref, *refs):
    pieces, (w_ref, cosine_ref, sine_ref, kv_ref, inverse_ref, held, sems) = refs[:8], refs[8:]
    rows, wide = pieces[0].shape
    width = held.shape[2]
    copies = weight_copies(tp_ref, w_ref, held, sems, 0, range(4))
    total = jnp.zeros((2 * rows, width), jnp.float32)
    squares = jnp.zeros((2 * rows, width), jnp.float32)
    for k in range(4):
        for c in range(wide // width):
            cut = slice(c * width, (c + 1) * width)
            chunk = jnp.concatenate([pieces[k][:, cut], pieces[4 + k][:, cut]], axis=0)
            chunk = chunk.astype(jnp.float32)
            squares += chunk * chunk
    for k in range(4):
        copies[k].wait()
        x = jnp.concatenate([pieces[k][...], pieces[4 + k][...]], axis=0)
        total += jnp.dot(x, held[k], preferred_element_type=jnp.float32)
    mean = jnp.sum(squares, axis=1, keepdims=True) * (1.0 / (4 * wide))
    inverse = jnp.broadcast_to(lax.rsqrt(mean + EPS), inverse_ref.shape)
    inverse_ref[...] = inverse
    kv_ref[...] = turned(total * inverse, cosine_ref[...], sine_ref[...]).astype(kv_ref.dtype)


def query_kernel(tp_ref, *refs):
    pieces, (w_ref, cosine_ref, sine_ref, inverse_ref, query_ref, total, held, sems) = (
        refs[:8],
        refs[8:],
    )
    copies = weight_copies(tp_ref, w_ref, held, sems, 0, range(4))
    for k in range(4):
        copies[k].wait()
        x = jnp.concatenate([pieces[k][...], pieces[4 + k][...]], axis=0)
        part = jnp.dot(x, held[k], preferred_element_type=jnp.float32)
        total[...] = part if k == 0 else total[...] + part
    for h in range(total.shape[1] // HEAD_DIM):
        cut = slice(h * HEAD_DIM, (h + 1) * HEAD_DIM)
        head = total[:, cut] * inverse_ref[...]
        query_ref[:, cut] = turned(head, cosine_ref[...], sine_ref[...]).astype(query_ref.dtype)


SCALAR = pl.BlockSpec(memory_space=pltpu.SMEM)
FAR = pl.BlockSpec(memory_space=pltpu.HBM)


def project_kv(tp, pieces, weights, cosine, sine):
    rows, wide = pieces[0].shape
    width = HEAD_DIM
    return pl.pallas_call(
        kv_kernel,
        out_shape=(
            jax.ShapeDtypeStruct((2 * rows, width), jnp.bfloat16),
            jax.ShapeDtypeStruct((2 * rows, width), jnp.float32),
        ),
        in_specs=[SCALAR] + [WHOLE] * 8 + [FAR] + [WHOLE] * 2,
        out_specs=(WHOLE, WHOLE),
        scratch_shapes=[
            pltpu.VMEM((4, wide, width), jnp.bfloat16),
            pltpu.SemaphoreType.DMA((4,)),
        ],
        cost_estimate=pl.CostEstimate(
            flops=16 * rows * wide * width,
            bytes_accessed=8 * wide * (rows * 2 + width),
            transcendentals=0,
        ),
        compiler_params=pltpu.CompilerParams(vmem_limit_bytes=8 << 20),
        name="project_kv",
    )(tp, *pieces, weights, cosine, sine)


def project_query(tp, pieces, weights, cosine, sine, inverse):
    rows, wide = pieces[0].shape
    width = weights.shape[1]
    return pl.pallas_call(
        query_kernel,
        out_shape=jax.ShapeDtypeStruct((2 * rows, width), jnp.bfloat16),
        in_specs=[SCALAR] + [WHOLE] * 8 + [FAR] + [WHOLE] * 3,
        out_specs=WHOLE,
        scratch_shapes=[
            pltpu.VMEM((2 * rows, width), jnp.float32),
            pltpu.VMEM((4, wide, width), jnp.bfloat16),
            pltpu.SemaphoreType.DMA((4,)),
        ],
        cost_estimate=pl.CostEstimate(
            flops=16 * rows * wide * width,
            bytes_accessed=8 * wide * (rows * 2 + width),
            transcendentals=0,
        ),
        compiler_params=pltpu.CompilerParams(vmem_limit_bytes=12 << 20),
        name="project_query",
    )(tp, *pieces, weights, cosine, sine, inverse)


def head_cut(h):
    return pl.ds(pl.multiple_of(h * HEAD_DIM, HEAD_DIM), HEAD_DIM)


def masked_scores(q, key, kpos, qpos):
    s = lax.dot_general(q, key, (((1,), (1,)), ((), ())), preferred_element_type=jnp.float32)
    return jnp.where(kpos <= qpos, s, NEGATIVE)


def first_kernel(q_ref, qpos_ref, kpos_ref, *refs):
    blocks, (mixed_ref, top_ref, sum_ref, scores) = refs[:7], refs[7:]
    span = blocks[0].shape[0]
    keys = [block[:, :HEAD_DIM] for block in blocks]
    values = [block[:, HEAD_DIM:] for block in blocks]
    qpos = qpos_ref[:, :1]

    def one_head(h, carry):
        cut = head_cut(h)
        q = q_ref[:, cut]
        top = None
        for b, key in enumerate(keys):
            s = masked_scores(q, key, kpos_ref[:, b * span : (b + 1) * span], qpos)
            scores[:, b * span : (b + 1) * span] = s
            top = s if top is None else jnp.maximum(top, s)
        top = jnp.max(top, axis=1, keepdims=True)
        mixed, total = None, None
        for b, value in enumerate(values):
            p = jnp.exp2(scores[:, b * span : (b + 1) * span] - top)
            part = jnp.dot(p.astype(value.dtype), value, preferred_element_type=jnp.float32)
            mixed = part if mixed is None else mixed + part
            total = p if total is None else total + p
        mixed_ref[:, cut] = mixed
        shape = (mixed.shape[0], HEAD_DIM)
        top_ref[:, cut] = jnp.broadcast_to(top, shape)
        sum_ref[:, cut] = jnp.broadcast_to(jnp.sum(total, axis=1, keepdims=True), shape)
        return carry

    lax.fori_loop(0, q_ref.shape[1] // HEAD_DIM, one_head, 0)


def last_kernel(core_ref, q_ref, qpos_ref, kpos_ref, *refs):
    mine_ref, other_ref, mixed_ref, top_ref, sum_ref, out_ref = refs
    first_core = core_ref[0] == 0
    mine, other = mine_ref[...], other_ref[...]
    key = jnp.where(first_core, mine, other)
    value = jnp.where(first_core, other, mine)
    span = mine.shape[0]
    kpos = kpos_ref[:, 7 * span :]
    qpos = qpos_ref[:, :1]

    def one_head(h, carry):
        cut = head_cut(h)
        s = masked_scores(q_ref[:, cut], key, kpos, qpos)
        old = top_ref[:, cut]
        new = jnp.maximum(old, jnp.max(s, axis=1, keepdims=True))
        p = jnp.exp2(s - new[:, :1])
        scale = jnp.exp2(old - new)
        part = jnp.dot(p.astype(value.dtype), value, preferred_element_type=jnp.float32)
        total = sum_ref[:, cut] * scale + jnp.sum(p, axis=1, keepdims=True)
        out_ref[:, cut] = ((mixed_ref[:, cut] * scale + part) / total).astype(out_ref.dtype)
        return carry

    lax.fori_loop(0, q_ref.shape[1] // HEAD_DIM, one_head, 0)


def attend_first(queries, qpos, kpos, blocks):
    rows, width = queries.shape
    span = 7 * blocks[0].shape[0]
    return pl.pallas_call(
        first_kernel,
        out_shape=[jax.ShapeDtypeStruct((rows, width), jnp.float32)] * 3,
        in_specs=[WHOLE] * (3 + 7),
        out_specs=[WHOLE] * 3,
        scratch_shapes=[pltpu.VMEM((rows, span), jnp.float32)],
        cost_estimate=pl.CostEstimate(
            flops=4 * rows * width * span,
            bytes_accessed=14 * rows * width + 4 * span * HEAD_DIM,
            transcendentals=rows * width // HEAD_DIM * span,
        ),
        compiler_params=pltpu.CompilerParams(vmem_limit_bytes=14 << 20),
        name="attend_first",
    )(queries, qpos, kpos, *blocks)


def attend_last(core, queries, qpos, kpos, halves, partial):
    rows, width = queries.shape
    span = halves[0].shape[0]
    return pl.pallas_call(
        last_kernel,
        out_shape=jax.ShapeDtypeStruct(queries.shape, jnp.bfloat16),
        in_specs=[SCALAR] + [WHOLE] * (3 + 2 + 3),
        out_specs=WHOLE,
        cost_estimate=pl.CostEstimate(
            flops=4 * rows * width * span,
            bytes_accessed=16 * rows * width + 4 * span * HEAD_DIM,
            transcendentals=rows * width // HEAD_DIM * span,
        ),
        compiler_params=pltpu.CompilerParams(vmem_limit_bytes=12 << 20),
        name="attend_last",
    )(core, queries, qpos, kpos, *halves, *partial)


def out_kernel(odd, tp_ref, attended_ref, w_ref, out_ref, held, sems):
    wide = held.shape[1]
    copies = weight_copies(tp_ref, w_ref, held, sems, 0, (odd, 2 + odd))
    for place in range(2):
        copies[place].wait()
        part = lax.dot_general(
            attended_ref[...],
            held[place],
            (((1,), (1,)), ((), ())),
            preferred_element_type=jnp.float32,
        )
        out_ref[:, place * wide : (place + 1) * wide] = part.astype(out_ref.dtype)


def project_out(tp, attended, weights, wide, odd):
    rows, half = attended.shape
    return pl.pallas_call(
        functools.partial(out_kernel, odd),
        out_shape=jax.ShapeDtypeStruct((rows, 2 * wide), jnp.bfloat16),
        in_specs=[SCALAR, WHOLE, FAR],
        out_specs=WHOLE,
        scratch_shapes=[
            pltpu.VMEM((2, wide, half), jnp.bfloat16),
            pltpu.SemaphoreType.DMA((2,)),
        ],
        cost_estimate=pl.CostEstimate(
            flops=4 * rows * wide * half,
            bytes_accessed=4 * wide * half + 4 * wide * rows + 2 * rows * half,
            transcendentals=0,
        ),
        compiler_params=pltpu.CompilerParams(vmem_limit_bytes=8 << 20),
        name="project_out",
    )(tp, attended, weights)


def along_z(x, by):
    return moved(x, lambda z, xh, xl, core: ((z + by) % Z, xh, xl, core))


def place_kernel(places, size, cuts, z_ref, *refs):
    outs, sems = refs[-1 - len(cuts) : -1], refs[-1]
    pieces = refs[-1 - len(cuts) - len(places) : -1 - len(cuts)]
    copies = []
    for (far, first), piece in zip(places, pieces):
        start = lax.rem(z_ref[0] + (far + Z), Z) * size + first
        rows = pl.ds(pl.multiple_of(start, size // 4), piece.shape[0])
        for (low, high), out in zip(cuts, outs):
            copies.append(
                pltpu.make_async_copy(
                    piece.at[:, pl.ds(low, high - low)], out.at[rows, :], sems.at[len(copies)]
                )
            )
            copies[-1].start()
    for copy in copies:
        copy.wait()


def placed(z, held, pieces, size, cuts):
    anywhere = pl.BlockSpec(memory_space=pl.ANY)
    dtype = pieces[0][2].dtype
    return pl.pallas_call(
        functools.partial(place_kernel, [piece[:2] for piece in pieces], size, cuts),
        out_shape=[jax.ShapeDtypeStruct((Z * size, high - low), dtype) for low, high in cuts],
        in_specs=[SCALAR] + [anywhere] * len(held) + [WHOLE] * len(pieces),
        out_specs=[anywhere] * len(cuts),
        scratch_shapes=[pltpu.SemaphoreType.DMA((len(pieces) * len(cuts),))],
        input_output_aliases={1 + i: i for i in range(len(held))},
        cost_estimate=pl.CostEstimate(
            flops=0,
            bytes_accessed=sum(4 * piece[2].size for piece in pieces),
            transcendentals=0,
        ),
        compiler_params=pltpu.CompilerParams(vmem_limit_bytes=6 << 20),
        name="placed",
    )(z, *held, *[piece[2] for piece in pieces])


def ring_gather(z, block, cuts):
    size = block.shape[0] // 2
    tips, held = [], []
    near = []
    for first in (0, size):
        chunk = block[first : first + size]
        tips.append((first, chunk, chunk))
        near.append((0, first, chunk))
    for hop in (1, 2, 3):
        tips = [
            (first, along_z(up, 1), along_z(down, -1)) for first, up, down in tips
        ]
        for first, up, down in tips:
            near += [(-hop, first, up), (hop, first, down)]
        held = placed(z, held, near, 2 * size, cuts)
        near = []
    middle = size // 2
    for first, up, down in tips:
        near.append((-4, first, along_z(up[:middle], 1)))
        near.append((4, first + middle, along_z(down[middle:], -1)))
    return placed(z, held, near, 2 * size, cuts), [tip[1:] for tip in tips]


def angle_tables(positions):
    half_width = HEAD_DIM // 2
    frequency = ROPE_BASE ** (-(jnp.arange(half_width, dtype=jnp.float32) * 2.0) / HEAD_DIM)
    angles = positions.astype(jnp.float32)[:, None] * frequency[None, :]
    return (jnp.cos(angles), jnp.sin(angles))


def row_positions(block_table, row_ids):
    slot_ids = row_ids // BLOCK
    matches = slot_ids[:, None] == jnp.arange(block_table.shape[0], dtype=jnp.int32)[None, :]
    owners = jnp.sum(jnp.where(matches, block_table[None, :], 0), axis=1)
    return owners * BLOCK + row_ids % BLOCK


def on_device(hidden_in, fresh_in, block_table, norm_gain, w_query, w_key, w_value, w_out):
    rows, wide = hidden_in.shape[1:]
    depth = w_query.shape[1]
    half = w_query.shape[2] // 2
    sections = lax.axis_size("section")
    z, xh, xl, core = (lax.axis_index(name) for name in PLANE)
    tp = 2 * xl + core
    last_section = lax.axis_index("section") == sections - 1
    first_core, first_xh = core == 0, xh == 0
    tp_scalar, core_scalar, z_scalar = (i.astype(jnp.int32).reshape(1) for i in (tp, core, z))
    (
        w_query,
        norm_gain,
        last_section,
        first_core,
        first_xh,
        tp_scalar,
        core_scalar,
        z_scalar,
    ) = lax.optimization_barrier(
        (
            w_query,
            norm_gain,
            last_section,
            first_core,
            first_xh,
            tp_scalar,
            core_scalar,
            z_scalar,
        )
    )

    gain = lax.dynamic_slice_in_dim(norm_gain[0], (2 * z + xh) * depth, depth)[:, None]

    def exchanged(zero, one):
        first = moved(jnp.where(first_xh, zero, one), lambda z, xh, xl, core: (z, xl, core, xh))
        second = moved(jnp.where(first_xh, one, zero), lambda z, xh, xl, core: (z, xl, core, 1 - xh))
        return jnp.where(
            first_core,
            jnp.concatenate([first, second], axis=0),
            jnp.concatenate([second, first], axis=0),
        )

    def scaled(wq, wkv):
        joined = jnp.concatenate([wq, wkv], axis=1).astype(jnp.float32) * gain
        return joined.astype(jnp.bfloat16)

    qkv_block = exchanged(
        scaled(w_query[0][:, :half], w_key[0]), scaled(w_query[0][:, half:], w_value[0])
    )

    def plane_rows(plane):
        ids = jnp.arange(rows, dtype=jnp.int32)
        return jnp.concatenate(
            [(2 * plane + xh) * rows + ids, (2 * plane + (1 - xh)) * rows + ids]
        )

    positions = row_positions(block_table, plane_rows(z))
    toward = 1 - 2 * core
    steps = [0, toward, 2 * toward, 3 * toward, -toward, -2 * toward, -3 * toward, 4]
    key_positions = row_positions(
        block_table, jnp.concatenate([plane_rows((z + by + Z) % Z) for by in steps])
    )
    key_positions = key_positions[None, :]
    query_positions = jnp.broadcast_to(positions[:, None], (2 * rows, HEAD_DIM))
    cosine_table, sine_table = angle_tables(positions)
    cosine_table = jnp.concatenate([cosine_table, cosine_table], axis=1)
    sine_table = jnp.concatenate([-sine_table, sine_table], axis=1)
    score_scale = HEAD_DIM ** (-0.5) * LOG2_E
    query_cosine, query_sine = cosine_table * score_scale, sine_table * score_scale
    kv_cosine = jnp.where(first_core, cosine_table, 1.0)
    kv_sine = jnp.where(first_core, sine_table, 0.0)
    tables = (
        query_positions, key_positions, query_cosine, query_sine, kv_cosine, kv_sine
    )
    qkv_block, out_source, tables = lax.optimization_barrier((qkv_block, w_out[0], tables))
    query_positions, key_positions, query_cosine, query_sine, kv_cosine, kv_sine = tables
    (query_weights, kv_weights), thirds = ring_gather(
        z_scalar, qkv_block, [(0, half), (half, half + HEAD_DIM)]
    )
    out_block = exchanged(out_source[:, :half], out_source[:, half:])
    out_block, _ = lax.optimization_barrier((out_block, thirds))
    (out_weights,), _ = ring_gather(z_scalar, out_block, [(0, half)])

    ring = [(i, (i + 1) % sections) for i in range(sections)]

    produced = []
    current = hidden_in[0]
    for step_index in range(sections):
        near = swap_core(current)
        by_l, by_h, by_hl = swap_x(current, 0, 1), swap_x(current, 1, 0), swap_x(current, 1, 1)
        far_l, far_h, far_hl = swap_core(by_l), swap_core(by_h), swap_core(by_hl)
        x = [current, near, by_l, far_l, by_h, far_h, by_hl, far_hl]
        kv, inverse = project_kv(tp_scalar, x, kv_weights, kv_cosine, kv_sine)
        opposite = moved(kv, lambda z, xh, xl, core: ((z + Z // 2) % Z, xh, xl, core))
        partner = swap_core(kv)
        own_block = jnp.where(
            first_core,
            jnp.concatenate([kv, partner], axis=1),
            jnp.concatenate([partner, kv], axis=1),
        )
        fetched = []
        for by in (1, 2, 3):
            fetched.append(from_z(own_block, by))
        queries = project_query(tp_scalar, x, query_weights, query_cosine, query_sine, inverse)
        blocks = [own_block] + fetched + [swap_core(block) for block in fetched]
        halves = [opposite, swap_core(opposite)]
        partial = attend_first(queries, query_positions, key_positions, blocks)
        attended = attend_last(
            core_scalar, queries, query_positions, key_positions, halves, partial
        )
        leaving = project_out(tp_scalar, attended, out_weights, wide, 1)
        arrived = swap_core(leaving)
        staying = project_out(tp_scalar, attended, out_weights, wide, 0)
        paired = staying.astype(jnp.float32) + arrived.astype(jnp.float32)
        own = paired[:rows, :wide]
        sent = paired.astype(jnp.bfloat16)
        from_l = swap_x(sent[:rows, wide:], 0, 1)
        from_h = swap_x(sent[rows:, :wide], 1, 0)
        from_hl = swap_x(sent[rows:, wide:], 1, 1)
        summed = (own + from_l.astype(jnp.float32)) + (
            from_h.astype(jnp.float32) + from_hl.astype(jnp.float32)
        )
        result = (current.astype(jnp.float32) + summed).astype(jnp.bfloat16)
        produced.append(result)
        if step_index + 1 < sections:
            onward = jnp.where(last_section, fresh_in[step_index], result)
            current = lax.ppermute(onward, "section", ring)
    return jnp.stack(produced)[:, None]


def solution(mesh):
    split = Mesh(
        mesh.devices.reshape(mesh.devices.shape[0], Z, XH, XL, CORE), ("section",) + PLANE
    )
    rows, columns = ("z", "xh"), ("xl", "core")
    in_specs = (
        P("section", rows, columns),
        P(None, rows, columns),
        P(),
        P("section", None),
        P("section", rows, columns),
        P("section", rows, columns),
        P("section", rows, columns),
        P("section", rows, columns),
    )
    out_specs = P(None, "section", rows, columns)
    return jax.shard_map(
        on_device, mesh=split, in_specs=in_specs, out_specs=out_specs, check_vma=False
    )
```

```python
import functools

import jax
import jax.numpy as jnp
from jax import lax
from jax.experimental import pallas as pl
from jax.experimental.pallas import tpu as pltpu
from jax.sharding import Mesh, PartitionSpec as P


HEAD_DIM = 128
BLOCK = 64


EPS = 1e-05
ROPE_BASE = 500000.0
NEGATIVE = -1e30
LOG2_E = 1.4426950408889634
Z, XH, XL, CORE = 8, 2, 2, 2
PLANE = ("z", "xh", "xl", "core")


def moved(x, target):
    def flat(z, xh, xl, core):
        return ((z * XH + xh) * XL + xl) * CORE + core

    pairs = [
        (flat(z, xh, xl, core), flat(*target(z, xh, xl, core)))
        for z in range(Z)
        for xh in range(XH)
        for xl in range(XL)
        for core in range(CORE)
    ]
    return lax.ppermute(x, PLANE, pairs)


def swap_core(x):
    return moved(x, lambda z, xh, xl, core: (z, xh, xl, 1 - core))


def swap_x(x, dh, dl):
    return moved(x, lambda z, xh, xl, core: (z, xh ^ dh, xl ^ dl, core))


def from_z(x, by):
    return moved(x, lambda z, xh, xl, core: ((z - (1 - 2 * core) * by) % Z, xh, xl, core))


WHOLE = pl.BlockSpec(memory_space=pltpu.VMEM)


def turned(x, cosine, sine):
    return x * cosine + pltpu.roll(x, x.shape[-1] // 2, 1) * sine


def weight_copies(tp_ref, w_ref, held, sems, column, order):
    wide, width = held.shape[1:]
    copies = []
    for place, partner in enumerate(order):
        first = pl.multiple_of((tp_ref[0] ^ partner) * wide, wide)
        block = w_ref.at[pl.ds(first, wide), pl.ds(column, width)]
        copies.append(pltpu.make_async_copy(block, held.at[place], sems.at[place]))
    for copy in copies:
        copy.start()
    return copies


def kv_kernel(tp_ref, *refs):
    pieces, (w_ref, cosine_ref, sine_ref, kv_ref, inverse_ref, held, sems) = refs[:8], refs[8:]
    rows, wide = pieces[0].shape
    width = held.shape[2]
    copies = weight_copies(tp_ref, w_ref, held, sems, 0, range(4))
    total = jnp.zeros((2 * rows, width), jnp.float32)
    squares = jnp.zeros((2 * rows, width), jnp.float32)
    for k in range(4):
        for c in range(wide // width):
            cut = slice(c * width, (c + 1) * width)
            chunk = jnp.concatenate([pieces[k][:, cut], pieces[4 + k][:, cut]], axis=0)
            chunk = chunk.astype(jnp.float32)
            squares += chunk * chunk
    for k in range(4):
        copies[k].wait()
        x = jnp.concatenate([pieces[k][...], pieces[4 + k][...]], axis=0)
        total += jnp.dot(x, held[k], preferred_element_type=jnp.float32)
    mean = jnp.sum(squares, axis=1, keepdims=True) * (1.0 / (4 * wide))
    inverse = jnp.broadcast_to(lax.rsqrt(mean + EPS), inverse_ref.shape)
    inverse_ref[...] = inverse
    kv_ref[...] = turned(total * inverse, cosine_ref[...], sine_ref[...]).astype(kv_ref.dtype)


def query_kernel(tp_ref, *refs):
    pieces, (w_ref, cosine_ref, sine_ref, inverse_ref, query_ref, total, held, sems) = (
        refs[:8],
        refs[8:],
    )
    copies = weight_copies(tp_ref, w_ref, held, sems, 0, range(4))
    for k in range(4):
        copies[k].wait()
        x = jnp.concatenate([pieces[k][...], pieces[4 + k][...]], axis=0)
        part = jnp.dot(x, held[k], preferred_element_type=jnp.float32)
        total[...] = part if k == 0 else total[...] + part
    for h in range(total.shape[1] // HEAD_DIM):
        cut = slice(h * HEAD_DIM, (h + 1) * HEAD_DIM)
        head = total[:, cut] * inverse_ref[...]
        query_ref[:, cut] = turned(head, cosine_ref[...], sine_ref[...]).astype(query_ref.dtype)


SCALAR = pl.BlockSpec(memory_space=pltpu.SMEM)
FAR = pl.BlockSpec(memory_space=pltpu.HBM)


def project_kv(tp, pieces, weights, cosine, sine):
    rows, wide = pieces[0].shape
    width = HEAD_DIM
    return pl.pallas_call(
        kv_kernel,
        out_shape=(
            jax.ShapeDtypeStruct((2 * rows, width), jnp.bfloat16),
            jax.ShapeDtypeStruct((2 * rows, width), jnp.float32),
        ),
        in_specs=[SCALAR] + [WHOLE] * 8 + [FAR] + [WHOLE] * 2,
        out_specs=(WHOLE, WHOLE),
        scratch_shapes=[
            pltpu.VMEM((4, wide, width), jnp.bfloat16),
            pltpu.SemaphoreType.DMA((4,)),
        ],
        cost_estimate=pl.CostEstimate(
            flops=16 * rows * wide * width,
            bytes_accessed=8 * wide * (rows * 2 + width),
            transcendentals=0,
        ),
        compiler_params=pltpu.CompilerParams(vmem_limit_bytes=8 << 20),
        name="project_kv",
    )(tp, *pieces, weights, cosine, sine)


def project_query(tp, pieces, weights, cosine, sine, inverse):
    rows, wide = pieces[0].shape
    width = weights.shape[1]
    return pl.pallas_call(
        query_kernel,
        out_shape=jax.ShapeDtypeStruct((2 * rows, width), jnp.bfloat16),
        in_specs=[SCALAR] + [WHOLE] * 8 + [FAR] + [WHOLE] * 3,
        out_specs=WHOLE,
        scratch_shapes=[
            pltpu.VMEM((2 * rows, width), jnp.float32),
            pltpu.VMEM((4, wide, width), jnp.bfloat16),
            pltpu.SemaphoreType.DMA((4,)),
        ],
        cost_estimate=pl.CostEstimate(
            flops=16 * rows * wide * width,
            bytes_accessed=8 * wide * (rows * 2 + width),
            transcendentals=0,
        ),
        compiler_params=pltpu.CompilerParams(vmem_limit_bytes=12 << 20),
        name="project_query",
    )(tp, *pieces, weights, cosine, sine, inverse)


def attention_kernel(core_ref, q_ref, qpos_ref, kpos_ref, *refs):
    blocks, halves, (out_ref, scores) = refs[:7], refs[7:9], refs[9:]
    span = blocks[0].shape[0]
    first_core = core_ref[0] == 0
    mine, other = halves[0][...], halves[1][...]
    keys = [b[:, :HEAD_DIM] for b in blocks] + [jnp.where(first_core, mine, other)]
    values = [b[:, HEAD_DIM:] for b in blocks] + [jnp.where(first_core, other, mine)]
    qpos = qpos_ref[:, :1]

    def one_head(h, carry):
        cut = pl.ds(pl.multiple_of(h * HEAD_DIM, HEAD_DIM), HEAD_DIM)
        q = q_ref[:, cut]
        top = None
        for b, key in enumerate(keys):
            s = lax.dot_general(
                q, key, (((1,), (1,)), ((), ())), preferred_element_type=jnp.float32
            )
            s = jnp.where(kpos_ref[:, b * span : (b + 1) * span] <= qpos, s, NEGATIVE)
            scores[:, b * span : (b + 1) * span] = s
            top = s if top is None else jnp.maximum(top, s)
        top = jnp.max(top, axis=1, keepdims=True)
        mixed, total = None, None
        for b, value in enumerate(values):
            p = jnp.exp2(scores[:, b * span : (b + 1) * span] - top)
            part = jnp.dot(p.astype(value.dtype), value, preferred_element_type=jnp.float32)
            mixed = part if mixed is None else mixed + part
            total = p if total is None else total + p
        weight_sum = jnp.sum(total, axis=1, keepdims=True)
        out_ref[:, cut] = (mixed / weight_sum).astype(out_ref.dtype)
        return carry

    lax.fori_loop(0, q_ref.shape[1] // HEAD_DIM, one_head, 0)


def attend(core, queries, qpos, kpos, blocks, halves):
    rows, width = queries.shape
    span = kpos.shape[1]
    return pl.pallas_call(
        attention_kernel,
        out_shape=jax.ShapeDtypeStruct(queries.shape, jnp.bfloat16),
        in_specs=[SCALAR] + [WHOLE] * (3 + 7 + 2),
        out_specs=WHOLE,
        scratch_shapes=[pltpu.VMEM((rows, span), jnp.float32)],
        cost_estimate=pl.CostEstimate(
            flops=4 * rows * width * span,
            bytes_accessed=4 * rows * width + 4 * span * HEAD_DIM,
            transcendentals=rows * width // HEAD_DIM * span,
        ),
        compiler_params=pltpu.CompilerParams(vmem_limit_bytes=12 << 20),
        name="attend",
    )(core, queries, qpos, kpos, *blocks, *halves)


def out_kernel(odd, tp_ref, attended_ref, w_ref, out_ref, held, sems):
    wide = held.shape[1]
    copies = weight_copies(tp_ref, w_ref, held, sems, 0, (odd, 2 + odd))
    for place in range(2):
        copies[place].wait()
        part = lax.dot_general(
            attended_ref[...],
            held[place],
            (((1,), (1,)), ((), ())),
            preferred_element_type=jnp.float32,
        )
        out_ref[:, place * wide : (place + 1) * wide] = part.astype(out_ref.dtype)


def project_out(tp, attended, weights, wide, odd):
    rows, half = attended.shape
    return pl.pallas_call(
        functools.partial(out_kernel, odd),
        out_shape=jax.ShapeDtypeStruct((rows, 2 * wide), jnp.bfloat16),
        in_specs=[SCALAR, WHOLE, FAR],
        out_specs=WHOLE,
        scratch_shapes=[
            pltpu.VMEM((2, wide, half), jnp.bfloat16),
            pltpu.SemaphoreType.DMA((2,)),
        ],
        cost_estimate=pl.CostEstimate(
            flops=4 * rows * wide * half,
            bytes_accessed=4 * wide * half + 4 * wide * rows + 2 * rows * half,
            transcendentals=0,
        ),
        compiler_params=pltpu.CompilerParams(vmem_limit_bytes=8 << 20),
        name="project_out",
    )(tp, attended, weights)


def along_z(x, by):
    return moved(x, lambda z, xh, xl, core: ((z + by) % Z, xh, xl, core))


def place_kernel(places, size, cuts, z_ref, *refs):
    outs, sems = refs[-1 - len(cuts) : -1], refs[-1]
    pieces = refs[-1 - len(cuts) - len(places) : -1 - len(cuts)]
    copies = []
    for (far, first), piece in zip(places, pieces):
        start = lax.rem(z_ref[0] + (far + Z), Z) * size + first
        rows = pl.ds(pl.multiple_of(start, size // 4), piece.shape[0])
        for (low, high), out in zip(cuts, outs):
            copies.append(
                pltpu.make_async_copy(
                    piece.at[:, pl.ds(low, high - low)], out.at[rows, :], sems.at[len(copies)]
                )
            )
            copies[-1].start()
    for copy in copies:
        copy.wait()


def placed(z, held, pieces, size, cuts):
    anywhere = pl.BlockSpec(memory_space=pl.ANY)
    dtype = pieces[0][2].dtype
    return pl.pallas_call(
        functools.partial(place_kernel, [piece[:2] for piece in pieces], size, cuts),
        out_shape=[jax.ShapeDtypeStruct((Z * size, high - low), dtype) for low, high in cuts],
        in_specs=[SCALAR] + [anywhere] * len(held) + [WHOLE] * len(pieces),
        out_specs=[anywhere] * len(cuts),
        scratch_shapes=[pltpu.SemaphoreType.DMA((len(pieces) * len(cuts),))],
        input_output_aliases={1 + i: i for i in range(len(held))},
        cost_estimate=pl.CostEstimate(
            flops=0,
            bytes_accessed=sum(4 * piece[2].size for piece in pieces),
            transcendentals=0,
        ),
        compiler_params=pltpu.CompilerParams(vmem_limit_bytes=6 << 20),
        name="placed",
    )(z, *held, *[piece[2] for piece in pieces])


def ring_gather(z, block, cuts):
    size = block.shape[0] // 2
    tips, held = [], []
    near = []
    for first in (0, size):
        chunk = block[first : first + size]
        tips.append((first, chunk, chunk))
        near.append((0, first, chunk))
    for hop in (1, 2, 3):
        tips = [
            (first, along_z(up, 1), along_z(down, -1)) for first, up, down in tips
        ]
        for first, up, down in tips:
            near += [(-hop, first, up), (hop, first, down)]
        held = placed(z, held, near, 2 * size, cuts)
        near = []
    middle = size // 2
    for first, up, down in tips:
        near.append((-4, first, along_z(up[:middle], 1)))
        near.append((4, first + middle, along_z(down[middle:], -1)))
    return placed(z, held, near, 2 * size, cuts), [tip[1:] for tip in tips]


def angle_tables(positions):
    half_width = HEAD_DIM // 2
    frequency = ROPE_BASE ** (-(jnp.arange(half_width, dtype=jnp.float32) * 2.0) / HEAD_DIM)
    angles = positions.astype(jnp.float32)[:, None] * frequency[None, :]
    return (jnp.cos(angles), jnp.sin(angles))


def row_positions(block_table, row_ids):
    slot_ids = row_ids // BLOCK
    matches = slot_ids[:, None] == jnp.arange(block_table.shape[0], dtype=jnp.int32)[None, :]
    owners = jnp.sum(jnp.where(matches, block_table[None, :], 0), axis=1)
    return owners * BLOCK + row_ids % BLOCK


def on_device(hidden_in, fresh_in, block_table, norm_gain, w_query, w_key, w_value, w_out):
    rows, wide = hidden_in.shape[1:]
    depth = w_query.shape[1]
    half = w_query.shape[2] // 2
    sections = lax.axis_size("section")
    z, xh, xl, core = (lax.axis_index(name) for name in PLANE)
    tp = 2 * xl + core
    last_section = lax.axis_index("section") == sections - 1
    first_core, first_xh = core == 0, xh == 0
    tp_scalar, core_scalar, z_scalar = (i.astype(jnp.int32).reshape(1) for i in (tp, core, z))
    (
        w_query,
        norm_gain,
        last_section,
        first_core,
        first_xh,
        tp_scalar,
        core_scalar,
        z_scalar,
    ) = lax.optimization_barrier(
        (
            w_query,
            norm_gain,
            last_section,
            first_core,
            first_xh,
            tp_scalar,
            core_scalar,
            z_scalar,
        )
    )

    gain = lax.dynamic_slice_in_dim(norm_gain[0], (2 * z + xh) * depth, depth)[:, None]

    def exchanged(zero, one):
        first = moved(jnp.where(first_xh, zero, one), lambda z, xh, xl, core: (z, xl, core, xh))
        second = moved(jnp.where(first_xh, one, zero), lambda z, xh, xl, core: (z, xl, core, 1 - xh))
        return jnp.where(
            first_core,
            jnp.concatenate([first, second], axis=0),
            jnp.concatenate([second, first], axis=0),
        )

    def scaled(wq, wkv):
        joined = jnp.concatenate([wq, wkv], axis=1).astype(jnp.float32) * gain
        return joined.astype(jnp.bfloat16)

    qkv_block = exchanged(
        scaled(w_query[0][:, :half], w_key[0]), scaled(w_query[0][:, half:], w_value[0])
    )

    def plane_rows(plane):
        ids = jnp.arange(rows, dtype=jnp.int32)
        return jnp.concatenate(
            [(2 * plane + xh) * rows + ids, (2 * plane + (1 - xh)) * rows + ids]
        )

    positions = row_positions(block_table, plane_rows(z))
    toward = 1 - 2 * core
    steps = [0, toward, 2 * toward, 3 * toward, -toward, -2 * toward, -3 * toward, 4]
    key_positions = row_positions(
        block_table, jnp.concatenate([plane_rows((z + by + Z) % Z) for by in steps])
    )
    key_positions = key_positions[None, :]
    query_positions = jnp.broadcast_to(positions[:, None], (2 * rows, HEAD_DIM))
    cosine_table, sine_table = angle_tables(positions)
    cosine_table = jnp.concatenate([cosine_table, cosine_table], axis=1)
    sine_table = jnp.concatenate([-sine_table, sine_table], axis=1)
    score_scale = HEAD_DIM ** (-0.5) * LOG2_E
    query_cosine, query_sine = cosine_table * score_scale, sine_table * score_scale
    kv_cosine = jnp.where(first_core, cosine_table, 1.0)
    kv_sine = jnp.where(first_core, sine_table, 0.0)
    tables = (
        query_positions, key_positions, query_cosine, query_sine, kv_cosine, kv_sine
    )
    qkv_block, out_source, tables = lax.optimization_barrier((qkv_block, w_out[0], tables))
    query_positions, key_positions, query_cosine, query_sine, kv_cosine, kv_sine = tables
    (query_weights, kv_weights), thirds = ring_gather(
        z_scalar, qkv_block, [(0, half), (half, half + HEAD_DIM)]
    )
    out_block = exchanged(out_source[:, :half], out_source[:, half:])
    out_block, _ = lax.optimization_barrier((out_block, thirds))
    (out_weights,), _ = ring_gather(z_scalar, out_block, [(0, half)])

    ring = [(i, (i + 1) % sections) for i in range(sections)]

    produced = []
    current = hidden_in[0]
    for step_index in range(sections):
        near = swap_core(current)
        by_l, by_h, by_hl = swap_x(current, 0, 1), swap_x(current, 1, 0), swap_x(current, 1, 1)
        far_l, far_h, far_hl = swap_core(by_l), swap_core(by_h), swap_core(by_hl)
        x = [current, near, by_l, far_l, by_h, far_h, by_hl, far_hl]
        kv, inverse = project_kv(tp_scalar, x, kv_weights, kv_cosine, kv_sine)
        opposite = moved(kv, lambda z, xh, xl, core: ((z + Z // 2) % Z, xh, xl, core))
        partner = swap_core(kv)
        own_block = jnp.where(
            first_core,
            jnp.concatenate([kv, partner], axis=1),
            jnp.concatenate([partner, kv], axis=1),
        )
        fetched = []
        for by in (1, 2, 3):
            fetched.append(from_z(own_block, by))
        queries = project_query(tp_scalar, x, query_weights, query_cosine, query_sine, inverse)
        passed = [swap_core(block) for block in fetched]
        blocks = [own_block] + fetched + passed
        halves = [opposite, swap_core(opposite)]
        attended = attend(
            core_scalar, queries, query_positions, key_positions, blocks, halves
        )
        leaving = project_out(tp_scalar, attended, out_weights, wide, 1)
        arrived = swap_core(leaving)
        staying = project_out(tp_scalar, attended, out_weights, wide, 0)
        paired = staying.astype(jnp.float32) + arrived.astype(jnp.float32)
        own = paired[:rows, :wide]
        sent = paired.astype(jnp.bfloat16)
        from_l = swap_x(sent[:rows, wide:], 0, 1)
        from_h = swap_x(sent[rows:, :wide], 1, 0)
        from_hl = swap_x(sent[rows:, wide:], 1, 1)
        summed = (own + from_l.astype(jnp.float32)) + (
            from_h.astype(jnp.float32) + from_hl.astype(jnp.float32)
        )
        result = (current.astype(jnp.float32) + summed).astype(jnp.bfloat16)
        produced.append(result)
        if step_index + 1 < sections:
            onward = jnp.where(last_section, fresh_in[step_index], result)
            current = lax.ppermute(onward, "section", ring)
    return jnp.stack(produced)[:, None]


def solution(mesh):
    split = Mesh(
        mesh.devices.reshape(mesh.devices.shape[0], Z, XH, XL, CORE), ("section",) + PLANE
    )
    rows, columns = ("z", "xh"), ("xl", "core")
    in_specs = (
        P("section", rows, columns),
        P(None, rows, columns),
        P(),
        P("section", None),
        P("section", rows, columns),
        P("section", rows, columns),
        P("section", rows, columns),
        P("section", rows, columns),
    )
    out_specs = P(None, "section", rows, columns)
    return jax.shard_map(
        on_device, mesh=split, in_specs=in_specs, out_specs=out_specs, check_vma=False
    )
```
